32 devices in a mesh: dp: 8 (over z, y), mp: 4 (over x, core).
Axes of the slice: x: 2, y: 2, z: 4, core: 2. Of those that a mesh axis runs over, the one named last changes fastest.
Arguments:
- tokens: bfloat16 [2048, 2048], P('dp'), may hold values from -6 to 6
- out_grad: bfloat16 [2048, 2048], P('dp'), may hold values from -6 to 6
- master: float32 [2368, 3, 7168], P('dp', None, 'mp'), may hold values from -6 to 6
- moment_one: float32 [2368, 3, 7168], P('dp', None, 'mp'), may hold values from -6 to 6
- moment_two: float32 [2368, 3, 7168], P('dp', None, 'mp'), may hold values from 0.05 to 5
- old_offsets: int32 [9], replicated, may hold values from 0 to 2048, as said below
- new_offsets: int32 [9], replicated, may hold values from 0 to 2048, as said below
Outputs:
- new_master: float32 [2880, 3, 7168], P('dp', None, 'mp')
- new_moment_one: float32 [2880, 3, 7168], P('dp', None, 'mp')
- new_moment_two: float32 [2880, 3, 7168], P('dp', None, 'mp')
- layer_output: bfloat16 [2048, 2048], P('dp', 'mp')
The draws below stay inside these ranges and needn't reach their ends.
Inputs may be any that keep to these rules, and one draw needn't show every extreme that they name: non-decreasing, old_offsets[0] = 0 and old_offsets[8] = 2048; device p holds rows old_offsets[p] to old_offsets[p + 1] - 1 in its first slots; every device holds at least one and at most 296 rows, and some device exactly 296. non-decreasing, new_offsets[0] = 0 and new_offsets[8] = 2048; exactly one device holds no rows, its index at least 2 and at most 3; every other device holds at least one and at most 360 rows, some device exactly 360; a row's device in the new layout is its device in the old layout or the next one along dp.
All inputs are finite; a program needn't handle non-finite values.
Results may differ from the reference program's by a relative error of at most 0.014.
Values may be sent and summed in bfloat16 or wider, within the bound.
A program may use at most 256 MiB of HBM per device.

```python
import math
import jax
import jax.numpy as jnp
from jax import lax

FEATURE_WIDTH = 2048
FF = 7168
TOK_DEV = 256
TOKENS = 2048
SHARD = 256
MAX_SHIFT = 20
CAP_OLD = 296
CAP_NEW = 360
N_DP = 8
N_MP = 4


def full_layout(key):
    base_key = jax.random.fold_in(key, 11)
    lost_key, forced_key, wiggle_key = jax.random.split(base_key, 3)
    leaving = jax.random.randint(lost_key, (), 2, N_DP // 2, dtype=jnp.int32)
    forced = jax.random.randint(forced_key, (), 2, N_DP - 2, dtype=jnp.int32)
    device_ids = jnp.arange(N_DP + 1, dtype=jnp.int32)
    wiggle = jax.random.randint(wiggle_key, (N_DP + 1,), -1, 2, dtype=jnp.int32)
    free_bound = (device_ids > 0) & (device_ids < N_DP) & (device_ids != forced) & (device_ids != forced + 1)
    old_bounds = device_ids * SHARD
    old_bounds = old_bounds + jnp.where(device_ids == forced, -MAX_SHIFT, 0)
    old_bounds = old_bounds + jnp.where(device_ids == forced + 1, MAX_SHIFT, 0)
    old_bounds = (old_bounds + jnp.where(free_bound, wiggle, 0)).astype(jnp.int32)
    old_sizes = (old_bounds[1:] - old_bounds[:-1]).astype(jnp.int32)
    lost_size = jnp.sum(jnp.where(jnp.arange(N_DP, dtype=jnp.int32) == leaving, old_sizes, 0)).astype(jnp.int32)

    def carry_step(previous, inputs):
        position, size_before = inputs
        pushed = jnp.maximum(previous + size_before - CAP_NEW, 1)
        moved_rows = jnp.where(position < leaving, 1, jnp.where(position == leaving, 0, jnp.where(position == leaving + 1, lost_size, pushed))).astype(jnp.int32)
        return (moved_rows, moved_rows)
    final_moved, inner_moves = lax.scan(carry_step, jnp.zeros((), jnp.int32), (jnp.arange(1, N_DP, dtype=jnp.int32), old_sizes[:-1]))
    boundary_moves = jnp.concatenate([jnp.zeros((1,), jnp.int32), inner_moves, jnp.zeros((1,), jnp.int32)])
    new_bounds = (old_bounds - boundary_moves).astype(jnp.int32)
    return (old_bounds, new_bounds)


def draw_new_offsets(key, part):
    old_bounds, new_bounds = full_layout(key)
    return new_bounds


def draw_old_offsets(key, part):
    old_bounds, new_bounds = full_layout(key)
    return old_bounds


def spiked(values, stream_key, source, target, blocks, factor):
    def block_of(dim):
        return (jnp.arange(values.shape[dim]) // (values.shape[dim] // blocks)).reshape((-1,) + (1,) * (values.ndim - 1 - dim))

    first = jax.random.permutation(stream_key, blocks)[block_of(target)]
    other_side = (block_of(target) + blocks // 2) % blocks
    return jnp.where((block_of(source) == first) | (block_of(source) == other_side), factor * values, values)


def level_of(own_key, shape, cuts, low, high):
    factor_of, own = 1.0, jax.random.fold_in(own_key, 6)
    for axis_at, parts in cuts:
        steps = jnp.exp(jax.random.uniform(jax.random.fold_in(own, axis_at), (parts,), jnp.float32, low / len(cuts), high / len(cuts)))
        factor_of = factor_of * jnp.repeat(steps, shape[axis_at] // parts).reshape([-1 if axis == axis_at else 1 for axis in range(len(shape))])
    return factor_of


def normal_values(key, shape, width, bound, pieces=(), kind=jnp.bfloat16):
    loudness = level_of(key, shape, pieces, -0.22, 0.18) if pieces else 1.0
    values = jax.random.normal(key, shape, jnp.float32) * width * loudness
    return jnp.minimum(jnp.maximum(values, -bound), bound).astype(kind)


def noise_with(own_key, shape, scale, limit, cuts, heavy, kind=jnp.bfloat16):
    entries = scale * jax.random.normal(own_key, shape, jnp.float32)
    if cuts:
        entries = entries * level_of(own_key, shape, cuts, -0.22, 0.18)
    return jnp.clip(spiked(entries, jax.random.fold_in(own_key, 3), *heavy), -limit, limit).astype(kind)


def setup_inputs(seed: int = 0) -> dict:
    splits = jax.random.split(jax.random.key(seed), 8)
    tokens = noise_with(splits[0], (TOKENS, FEATURE_WIDTH), 1.0, 6.0, ((0, 8),), (0, 1, 8, 2.0))
    out_grad = normal_values(splits[1], (TOKENS, FEATURE_WIDTH), 1.0, 6.0, ((0, 8),))
    master = normal_values(splits[2], (N_DP * CAP_OLD, 3, FF), 1.0, 6.0, ((0, 8), (2, 4)), jnp.float32)
    moment_one = normal_values(splits[3], (N_DP * CAP_OLD, 3, FF), 1.0, 6.0, ((0, 8), (2, 4)), jnp.float32)
    moment_two = jnp.clip(jnp.exp(math.log(5.0) - 4.6051702 * jax.random.uniform(splits[4], (N_DP * CAP_OLD, 3, FF), jnp.float32) ** level_of(splits[4], (N_DP * CAP_OLD, 3, FF), ((0, 8), (2, 4)), -0.2, 0.2)), 0.05, 5.0)
    old_offsets = draw_old_offsets(jax.random.fold_in(splits[7], 71), 0)
    new_offsets = draw_new_offsets(jax.random.fold_in(splits[7], 71), 0)
    return dict(tokens=tokens, out_grad=out_grad, master=master, moment_one=moment_one, moment_two=moment_two, old_offsets=old_offsets, new_offsets=new_offsets)


beta_one = 0.9
beta_two = 0.95
learn_rate = 0.01
decay_rate = 0.1
adam_eps = 1e-08
bias_one = 1.0 - 0.9 ** 10
bias_two = 1.0 - 0.95 ** 10

def lookup(small_table, wanted):
    matches = wanted[..., None] == jnp.arange(small_table.shape[0], dtype=jnp.int32)
    return lax.optimization_barrier(jnp.sum(jnp.where(matches, small_table, 0), axis=-1)).astype(jnp.int32)

def unpack(packed, offsets, capacity):
    row_index = jnp.arange(FEATURE_WIDTH, dtype=jnp.int32)
    owner_index = lax.optimization_barrier(jnp.sum((offsets[1:N_DP][None, :] <= row_index[:, None]).astype(jnp.int32), axis=1)).astype(jnp.int32)
    slot_index = owner_index * capacity + row_index - lookup(offsets, owner_index)
    return jnp.take(packed, slot_index.astype(jnp.int32), axis=0)

def pack(full_rows, offsets, capacity):
    slot_index = jnp.arange(N_DP * capacity, dtype=jnp.int32)
    owner_index = slot_index // capacity
    local_index = slot_index - owner_index * capacity
    row_start = lookup(offsets, owner_index)
    in_range = local_index < lookup(offsets, owner_index + 1) - row_start
    row_index = jnp.clip(row_start + local_index, 0, FEATURE_WIDTH - 1).astype(jnp.int32)
    picked = jnp.take(full_rows, row_index, axis=0)
    return jnp.where(in_range[:, None, None, None], picked, 0.0)

def adam_step(master_rows, first_rows, second_rows, grads):
    first_new = beta_one * first_rows + (1.0 - beta_one) * grads
    second_new = beta_two * second_rows + (1.0 - beta_two) * grads * grads
    update = first_new / bias_one / (jnp.sqrt(second_new / bias_two) + adam_eps)
    master_new = master_rows - learn_rate * (update + decay_rate * master_rows)
    return (master_new, first_new, second_new)

def reference(tokens, out_grad, master, moment_one, moment_two, old_offsets, new_offsets):
    full_rows = unpack(jnp.stack([master, moment_one, moment_two], axis=1), old_offsets, CAP_OLD)
    weights = full_rows[:, 0].astype(jnp.bfloat16)
    gate_weight = weights[:, 0]
    up_weight = weights[:, 1]
    down_weight = weights[:, 2]
    scale_in = FEATURE_WIDTH ** (-0.5)
    scale_hidden = FF ** (-0.5)
    block_width = FF // N_MP
    down_blocks = down_weight.astype(jnp.float32).reshape(FEATURE_WIDTH, N_MP, block_width)
    live_flags = new_offsets[1:] != new_offsets[:-1]

    def one_group(grad_total, inputs):
        group_tokens, group_upstream, live_flag = inputs
        upstream = jnp.where(live_flag, group_upstream, jnp.zeros_like(group_upstream))
        gate_act = jnp.dot(group_tokens, gate_weight, preferred_element_type=jnp.float32) * scale_in
        up_act = jnp.dot(group_tokens, up_weight, preferred_element_type=jnp.float32) * scale_in
        sigmoid_gate = jax.nn.sigmoid(gate_act)
        hidden = (gate_act * sigmoid_gate * up_act).astype(jnp.bfloat16)
        hidden_blocks = hidden.astype(jnp.float32).reshape(TOK_DEV, N_MP, block_width)
        partial_value = jnp.einsum('tcf,dcf->ctd', hidden_blocks, down_blocks, precision=lax.Precision.HIGHEST) * scale_hidden
        partial_value = jnp.where(live_flag, partial_value, 0.0).astype(jnp.bfloat16)
        group_output = lax.optimization_barrier(jnp.sum(lax.optimization_barrier(partial_value).astype(jnp.float32), axis=0)).astype(jnp.bfloat16)
        back_grad = jnp.dot(upstream, down_weight, preferred_element_type=jnp.float32) * scale_hidden
        gate_grad = (back_grad * up_act * sigmoid_gate * (1.0 + gate_act * (1.0 - sigmoid_gate))).astype(jnp.bfloat16)
        up_grad = (back_grad * gate_act * sigmoid_gate).astype(jnp.bfloat16)
        term_rows = jnp.stack([jnp.dot(group_tokens.T, gate_grad, preferred_element_type=jnp.float32) * scale_in, jnp.dot(group_tokens.T, up_grad, preferred_element_type=jnp.float32) * scale_in, jnp.dot(upstream.T, hidden, preferred_element_type=jnp.float32) * scale_hidden], axis=1)
        rounded = lax.optimization_barrier(term_rows.astype(jnp.bfloat16)).astype(jnp.float32)
        return (grad_total + rounded, group_output)
    grad_total, outputs = lax.scan(one_group, jnp.zeros((FEATURE_WIDTH, 3, FF), jnp.float32), (tokens.reshape(N_DP, TOK_DEV, FEATURE_WIDTH), out_grad.reshape(N_DP, TOK_DEV, FEATURE_WIDTH), live_flags))
    new_rows = jnp.stack(adam_step(full_rows[:, 0], full_rows[:, 1], full_rows[:, 2], grad_total), axis=1)
    packed = pack(new_rows, new_offsets, CAP_NEW)
    return (packed[:, 0], packed[:, 1], packed[:, 2], outputs.reshape(TOKENS, FEATURE_WIDTH))
```

```python
import jax
import jax.numpy as jnp
from jax import lax
from jax.sharding import PartitionSpec as P

FEATURE_WIDTH = 2048
FF = 7168


beta_one = 0.9
beta_two = 0.95
learn_rate = 0.01
decay_rate = 0.1
adam_eps = 1e-08
bias_one = 1.0 - 0.9**10
bias_two = 1.0 - 0.95**10


def passed_along(value, axis, by):
    peers = lax.axis_size(axis)
    pairs = [(i, i + by) for i in range(peers) if 0 <= i + by < peers]
    return lax.ppermute(value, axis, pairs)


def lookup(small_table, wanted):
    matches = wanted[..., None] == jnp.arange(small_table.shape[0], dtype=jnp.int32)
    return jnp.sum(jnp.where(matches, small_table, 0), axis=-1)


def row_layout(row_count, capacity, offsets):
    row_index = jnp.arange(row_count, dtype=jnp.int32)
    owner_index = row_index // capacity
    local_index = row_index - owner_index * capacity
    row_start = lookup(offsets, owner_index)
    in_range = local_index < lookup(offsets, owner_index + 1) - row_start
    target = jnp.clip(row_start + local_index, 0, FEATURE_WIDTH - 1)
    return (target, in_range)


def adam_step(master_rows, first_rows, second_rows, grads):
    first_new = beta_one * first_rows + (1.0 - beta_one) * grads
    second_new = beta_two * second_rows + (1.0 - beta_two) * grads * grads
    update = first_new / bias_one / (jnp.sqrt(second_new / bias_two) + adam_eps)
    master_new = master_rows - learn_rate * (update + decay_rate * master_rows)
    return (master_new, first_new, second_new)


def reshard(states, old_offsets, new_offsets, capacity_new):
    capacity_old = states.shape[0]
    from_left = passed_along(states.astype(jnp.bfloat16), "dp", 1).astype(states.dtype)
    device_index = lax.axis_index("dp")
    local_index = jnp.arange(capacity_new, dtype=jnp.int32)
    row_start = lookup(new_offsets, device_index)
    row_count = lookup(new_offsets, device_index + 1) - row_start
    in_range = local_index < row_count
    row_index = jnp.clip(row_start + local_index, 0, FEATURE_WIDTH - 1)
    owner_index = jnp.sum(
        (old_offsets[1:-1][None, :] <= row_index[:, None]).astype(jnp.int32), axis=1
    )
    slot_index = (
        (owner_index - device_index + 1) * capacity_old
        + row_index
        - lookup(old_offsets, owner_index)
    )
    neighbours = jnp.concatenate([from_left, states], axis=0)
    picked = jnp.take(neighbours, slot_index, axis=0, mode="clip")
    return jnp.where(in_range[:, None, None, None], picked, 0.0)


def train_pass(tokens, upstream, weights, layout, capacity, live_flag):
    columns = weights.shape[2]
    scale_in = FEATURE_WIDTH ** (-0.5)
    scale_hidden = FF ** (-0.5)
    contract_rows = (((0,), (0,)), ((), ()))
    shard_piece = lax.all_gather(weights, "dp", axis=0, tiled=True)
    down_rows = jnp.zeros((FEATURE_WIDTH, columns), jnp.bfloat16)
    target, in_range = row_layout(shard_piece.shape[0], capacity, layout)
    shard_piece = jnp.where(in_range[:, None, None], shard_piece, jnp.zeros_like(shard_piece))
    token_columns = jnp.take(tokens, target, axis=1, mode="clip")
    upstream_columns = jnp.take(upstream, target, axis=1, mode="clip")
    gate_sum = jnp.dot(token_columns, shard_piece[:, 0], preferred_element_type=jnp.float32)
    up_sum = jnp.dot(token_columns, shard_piece[:, 1], preferred_element_type=jnp.float32)
    back_sum = jnp.dot(upstream_columns, shard_piece[:, 2], preferred_element_type=jnp.float32)
    placed = jnp.where(in_range, target, FEATURE_WIDTH)
    down_rows = down_rows.at[placed].set(shard_piece[:, 2], mode="drop")
    gate_sum, up_sum, back_sum, down_rows = (gate_sum, up_sum, back_sum, down_rows)
    gate_act = gate_sum * scale_in
    up_act = up_sum * scale_in
    back_grad = back_sum * scale_hidden
    sigmoid_gate = jax.nn.sigmoid(gate_act)
    hidden = (gate_act * sigmoid_gate * up_act).astype(jnp.bfloat16)
    partial_value = (
        lax.dot_general(
            hidden, down_rows, (((1,), (1,)), ((), ())), preferred_element_type=jnp.float32
        )
        * scale_hidden
    )
    partial_value = jnp.where(live_flag, partial_value, 0.0)
    layer_output = lax.psum_scatter(
        partial_value.astype(jnp.bfloat16), "mp", scatter_dimension=1, tiled=True
    )
    gate_grad = (
        back_grad * up_act * sigmoid_gate * (1.0 + gate_act * (1.0 - sigmoid_gate))
    ).astype(jnp.bfloat16)
    up_grad = (back_grad * gate_act * sigmoid_gate).astype(jnp.bfloat16)
    target, in_range = row_layout(lax.axis_size("dp") * capacity, capacity, layout)
    token_columns = jnp.take(tokens, target, axis=1, mode="clip")
    upstream_columns = jnp.take(upstream, target, axis=1, mode="clip")
    gate_part = (
        lax.dot_general(token_columns, gate_grad, contract_rows, preferred_element_type=jnp.float32)
        * scale_in
    )
    up_part = (
        lax.dot_general(token_columns, up_grad, contract_rows, preferred_element_type=jnp.float32)
        * scale_in
    )
    down_part = (
        lax.dot_general(upstream_columns, hidden, contract_rows, preferred_element_type=jnp.float32)
        * scale_hidden
    )
    stacked = jnp.stack([gate_part, up_part, down_part], axis=1)
    grads = lax.psum_scatter(
        jnp.where(in_range[:, None, None], stacked, 0.0).astype(jnp.bfloat16),
        "dp",
        scatter_dimension=0,
        tiled=True,
    ).astype(jnp.float32)
    return (grads, layer_output)


def body(tokens, out_grad, master, moment_one, moment_two, old_offsets, new_offsets):
    devices = lax.axis_size("dp")
    shard_rows = FEATURE_WIDTH // devices
    jitter_rows = shard_rows // (2 * (devices - 1)) + 2
    capacity_new = shard_rows + shard_rows // 4 + 2 * jitter_rows
    device_index = lax.axis_index("dp")
    live_flag = lookup(new_offsets, device_index + 1) != lookup(new_offsets, device_index)
    upstream = jnp.where(live_flag, out_grad, jnp.zeros_like(out_grad))
    states = jnp.stack([master, moment_one, moment_two], axis=1)
    weights = states[:, 0].astype(jnp.bfloat16)
    grads, layer_output = train_pass(
        tokens, upstream, weights, old_offsets, states.shape[0], live_flag
    )
    updated = jnp.stack(adam_step(states[:, 0], states[:, 1], states[:, 2], grads), axis=1)
    updated = reshard(updated, old_offsets, new_offsets, capacity_new)
    return (updated[:, 0], updated[:, 1], updated[:, 2], layer_output)


def grown(value, axis, before, after):
    widths = [(0, 0)] * value.ndim
    widths[axis] = (before, after)
    return jnp.pad(value, widths)


def token_pass(tokens, upstream, master, old_offsets, new_offsets, capacity_new):
    peers = lax.axis_size("dp")
    feature_peers = lax.axis_size("mp")
    capacity_old, kinds, columns = master.shape
    width = columns // peers
    features = tokens.shape[1]
    scale_in = features ** (-0.5)
    scale_hidden = (columns * feature_peers) ** (-0.5)

    piece = tokens.shape[0] // feature_peers
    first_row = lax.axis_index("mp") * piece
    mine = jnp.stack(
        [
            lax.dynamic_slice_in_dim(tokens, first_row, piece, 0),
            lax.dynamic_slice_in_dim(upstream, first_row, piece, 0),
        ]
    )
    everyone = lax.all_gather(mine, ("dp", "mp"), axis=1, tiled=True)
    all_tokens, all_upstream = everyone[0], everyone[1]

    weights = master.astype(jnp.bfloat16).transpose(1, 0, 2)
    weights = weights.reshape(kinds, capacity_old, peers, width).transpose(2, 0, 1, 3)
    blocks = lax.all_to_all(weights, "dp", 0, 0)
    rows = jnp.zeros((kinds, features + capacity_old, width), jnp.bfloat16)
    for peer in range(peers):
        rows = lax.dynamic_update_slice(rows, blocks[peer], (0, old_offsets[peer], 0))
    rows = rows[:, :features]

    def product(left, right, left_dim, right_dim):
        return lax.dot_general(
            left,
            right,
            (((left_dim,), (right_dim,)), ((), ())),
            preferred_element_type=jnp.float32,
        )

    gate_act = product(all_tokens, rows[0], 1, 0) * scale_in
    up_act = product(all_tokens, rows[1], 1, 0) * scale_in
    back_grad = product(all_upstream, rows[2], 1, 0) * scale_hidden
    sigmoid_gate = jax.nn.sigmoid(gate_act)
    hidden = (gate_act * sigmoid_gate * up_act).astype(jnp.bfloat16)
    gate_grad = (
        back_grad * up_act * sigmoid_gate * (1.0 + gate_act * (1.0 - sigmoid_gate))
    ).astype(jnp.bfloat16)
    up_grad = (back_grad * gate_act * sigmoid_gate).astype(jnp.bfloat16)

    grads = jnp.stack(
        [
            (product(all_tokens, gate_grad, 0, 0) * scale_in).astype(jnp.bfloat16),
            (product(all_tokens, up_grad, 0, 0) * scale_in).astype(jnp.bfloat16),
            (product(all_upstream, hidden, 0, 0) * scale_hidden).astype(jnp.bfloat16),
        ]
    )
    grads = grown(grads, 1, 0, capacity_new)
    packed = jnp.stack(
        [
            lax.dynamic_slice_in_dim(grads, new_offsets[peer], capacity_new, 1)
            for peer in range(peers)
        ]
    )
    packed = lax.all_to_all(packed, "dp", 0, 0)
    grads = packed.transpose(1, 2, 0, 3).reshape(kinds, capacity_new, columns)

    partial_value = (product(hidden, rows[2], 1, 1) * scale_hidden).astype(jnp.bfloat16)
    partial_value = lax.psum_scatter(partial_value, "mp", scatter_dimension=1, tiled=True)
    layer_output = lax.psum_scatter(partial_value, "dp", scatter_dimension=0, tiled=True)
    return grads.astype(jnp.float32), layer_output


def token_body(tokens, out_grad, master, moment_one, moment_two, old_offsets, new_offsets):
    devices = lax.axis_size("dp")
    capacity_old = master.shape[0]
    capacity_new = new_capacity(tokens.shape[1], devices)
    device_index = lax.axis_index("dp")
    new_start = lookup(new_offsets, device_index)
    new_end = lookup(new_offsets, device_index + 1)
    old_start = lookup(old_offsets, device_index)
    left_start = lookup(old_offsets, jnp.maximum(device_index - 1, 0))
    live_flag = new_end != new_start
    upstream = jnp.where(live_flag, out_grad, jnp.zeros_like(out_grad))

    states = [value.transpose(1, 0, 2) for value in (master, moment_one, moment_two)]
    from_left = [passed_along(value.astype(jnp.bfloat16), "dp", 1) for value in states]
    grads, layer_output = token_pass(
        tokens, upstream, master, old_offsets, new_offsets, capacity_new
    )
    arrived = jnp.clip(old_start - new_start, 0, capacity_new)
    left_skip = jnp.clip(new_start - left_start, 0, capacity_old)
    slot = jnp.arange(capacity_new, dtype=jnp.int32)[None, :, None]

    def placed(own, left):
        left = lax.dynamic_slice_in_dim(grown(left, 1, 0, capacity_new), left_skip, capacity_new, 1)
        own = grown(own, 1, capacity_new, capacity_new - capacity_old)
        own = lax.dynamic_slice_in_dim(own, capacity_new - arrived, capacity_new, 1)
        return jnp.where(slot < arrived, left.astype(jnp.float32), own)

    rows = [placed(own, left) for own, left in zip(states, from_left)]
    updated = adam_step(rows[0], rows[1], rows[2], grads)
    in_range = slot < new_end - new_start
    updated = [jnp.where(in_range, value, 0.0).transpose(1, 0, 2) for value in updated]
    layer_output = jnp.where(live_flag, layer_output, jnp.zeros_like(layer_output))
    return (updated[0], updated[1], updated[2], layer_output)


def new_capacity(features, devices):
    shard_rows = features // devices
    jitter_rows = shard_rows // (2 * (devices - 1)) + 2
    return shard_rows + shard_rows // 4 + 2 * jitter_rows


def any_body(tokens, out_grad, master, *others):
    devices = lax.axis_size("dp")
    columns = master.shape[2]
    moved_tokens = 3 * tokens.shape[0] * devices
    moved_rows = 2 * master.shape[1] * columns
    whole = columns % devices == 0 and tokens.shape[0] % lax.axis_size("mp") == 0
    chosen = token_body if whole and moved_tokens <= moved_rows else body
    return chosen(tokens, out_grad, master, *others)


def solution(mesh):
    placed = (
        P("dp", None),
        P("dp", None),
        P("dp", None, "mp"),
        P("dp", None, "mp"),
        P("dp", None, "mp"),
        P(),
        P(),
    )
    return jax.shard_map(
        any_body,
        mesh=mesh,
        in_specs=placed,
        out_specs=(P("dp", None, "mp"), P("dp", None, "mp"), P("dp", None, "mp"), P("dp", "mp")),
        check_vma=False,
    )
```

```python
import jax
import jax.numpy as jnp
from jax import lax
from jax.sharding import PartitionSpec as P


FEATURE_WIDTH = 2048
FF = 7168


beta_one = 0.9
beta_two = 0.95
learn_rate = 0.01
decay_rate = 0.1
adam_eps = 1e-08
bias_one = 1.0 - 0.9**10
bias_two = 1.0 - 0.95**10


def passed_along(value, axis, by):
    peers = lax.axis_size(axis)
    pairs = [(i, i + by) for i in range(peers) if 0 <= i + by < peers]
    return lax.ppermute(value, axis, pairs)


def lookup(small_table, wanted):
    matches = wanted[..., None] == jnp.arange(small_table.shape[0], dtype=jnp.int32)
    return jnp.sum(jnp.where(matches, small_table, 0), axis=-1)


def row_layout(row_count, capacity, offsets):
    row_index = jnp.arange(row_count, dtype=jnp.int32)
    owner_index = row_index // capacity
    local_index = row_index - owner_index * capacity
    row_start = lookup(offsets, owner_index)
    in_range = local_index < lookup(offsets, owner_index + 1) - row_start
    target = jnp.clip(row_start + local_index, 0, FEATURE_WIDTH - 1)
    return (target, in_range)


def adam_step(master_rows, first_rows, second_rows, grads):
    first_new = beta_one * first_rows + (1.0 - beta_one) * grads
    second_new = beta_two * second_rows + (1.0 - beta_two) * grads * grads
    update = first_new / bias_one / (jnp.sqrt(second_new / bias_two) + adam_eps)
    master_new = master_rows - learn_rate * (update + decay_rate * master_rows)
    return (master_new, first_new, second_new)


def reshard(states, old_offsets, new_offsets, capacity_new):
    capacity_old = states.shape[0]
    from_left = passed_along(states.astype(jnp.bfloat16), "dp", 1).astype(states.dtype)
    device_index = lax.axis_index("dp")
    local_index = jnp.arange(capacity_new, dtype=jnp.int32)
    row_start = lookup(new_offsets, device_index)
    row_count = lookup(new_offsets, device_index + 1) - row_start
    in_range = local_index < row_count
    row_index = jnp.clip(row_start + local_index, 0, FEATURE_WIDTH - 1)
    owner_index = jnp.sum(
        (old_offsets[1:-1][None, :] <= row_index[:, None]).astype(jnp.int32), axis=1
    )
    slot_index = (
        (owner_index - device_index + 1) * capacity_old
        + row_index
        - lookup(old_offsets, owner_index)
    )
    neighbours = jnp.concatenate([from_left, states], axis=0)
    picked = jnp.take(neighbours, slot_index, axis=0, mode="clip")
    return jnp.where(in_range[:, None, None, None], picked, 0.0)


def train_pass(tokens, upstream, weights, layout, capacity, live_flag):
    columns = weights.shape[2]
    scale_in = FEATURE_WIDTH ** (-0.5)
    scale_hidden = FF ** (-0.5)
    contract_rows = (((0,), (0,)), ((), ()))
    shard_piece = lax.all_gather(weights, "dp", axis=0, tiled=True)
    down_rows = jnp.zeros((FEATURE_WIDTH, columns), jnp.bfloat16)
    target, in_range = row_layout(shard_piece.shape[0], capacity, layout)
    shard_piece = jnp.where(in_range[:, None, None], shard_piece, jnp.zeros_like(shard_piece))
    token_columns = jnp.take(tokens, target, axis=1, mode="clip")
    upstream_columns = jnp.take(upstream, target, axis=1, mode="clip")
    gate_sum = jnp.dot(token_columns, shard_piece[:, 0], preferred_element_type=jnp.float32)
    up_sum = jnp.dot(token_columns, shard_piece[:, 1], preferred_element_type=jnp.float32)
    back_sum = jnp.dot(upstream_columns, shard_piece[:, 2], preferred_element_type=jnp.float32)
    placed = jnp.where(in_range, target, FEATURE_WIDTH)
    down_rows = down_rows.at[placed].set(shard_piece[:, 2], mode="drop")
    gate_sum, up_sum, back_sum, down_rows = (gate_sum, up_sum, back_sum, down_rows)
    gate_act = gate_sum * scale_in
    up_act = up_sum * scale_in
    back_grad = back_sum * scale_hidden
    sigmoid_gate = jax.nn.sigmoid(gate_act)
    hidden = (gate_act * sigmoid_gate * up_act).astype(jnp.bfloat16)
    partial_value = (
        lax.dot_general(
            hidden, down_rows, (((1,), (1,)), ((), ())), preferred_element_type=jnp.float32
        )
        * scale_hidden
    )
    partial_value = jnp.where(live_flag, partial_value, 0.0)
    layer_output = lax.psum_scatter(
        partial_value.astype(jnp.bfloat16), "mp", scatter_dimension=1, tiled=True
    )
    gate_grad = (
        back_grad * up_act * sigmoid_gate * (1.0 + gate_act * (1.0 - sigmoid_gate))
    ).astype(jnp.bfloat16)
    up_grad = (back_grad * gate_act * sigmoid_gate).astype(jnp.bfloat16)
    target, in_range = row_layout(lax.axis_size("dp") * capacity, capacity, layout)
    token_columns = jnp.take(tokens, target, axis=1, mode="clip")
    upstream_columns = jnp.take(upstream, target, axis=1, mode="clip")
    gate_part = (
        lax.dot_general(token_columns, gate_grad, contract_rows, preferred_element_type=jnp.float32)
        * scale_in
    )
    up_part = (
        lax.dot_general(token_columns, up_grad, contract_rows, preferred_element_type=jnp.float32)
        * scale_in
    )
    down_part = (
        lax.dot_general(upstream_columns, hidden, contract_rows, preferred_element_type=jnp.float32)
        * scale_hidden
    )
    stacked = jnp.stack([gate_part, up_part, down_part], axis=1)
    grads = lax.psum_scatter(
        jnp.where(in_range[:, None, None], stacked, 0.0).astype(jnp.bfloat16),
        "dp",
        scatter_dimension=0,
        tiled=True,
    ).astype(jnp.float32)
    return (grads, layer_output)


def body(tokens, out_grad, master, moment_one, moment_two, old_offsets, new_offsets):
    devices = lax.axis_size("dp")
    shard_rows = FEATURE_WIDTH // devices
    jitter_rows = shard_rows // (2 * (devices - 1)) + 2
    capacity_new = shard_rows + shard_rows // 4 + 2 * jitter_rows
    device_index = lax.axis_index("dp")
    live_flag = lookup(new_offsets, device_index + 1) != lookup(new_offsets, device_index)
    upstream = jnp.where(live_flag, out_grad, jnp.zeros_like(out_grad))
    states = jnp.stack([master, moment_one, moment_two], axis=1)
    weights = states[:, 0].astype(jnp.bfloat16)
    grads, layer_output = train_pass(
        tokens, upstream, weights, old_offsets, states.shape[0], live_flag
    )
    updated = jnp.stack(adam_step(states[:, 0], states[:, 1], states[:, 2], grads), axis=1)
    updated = reshard(updated, old_offsets, new_offsets, capacity_new)
    return (updated[:, 0], updated[:, 1], updated[:, 2], layer_output)


def grown(value, axis, before, after):
    widths = [(0, 0)] * value.ndim
    widths[axis] = (before, after)
    return jnp.pad(value, widths)


def lane_split(columns, peers):
    return -(-columns // (peers * 128)) * 128


def product(left, right, left_dim, right_dim):
    return lax.dot_general(
        left,
        right,
        (((left_dim,), (right_dim,)), ((), ())),
        preferred_element_type=jnp.float32,
    )


def token_pass(tokens, upstream, master, old_offsets, new_offsets, capacity_new):
    peers = lax.axis_size("dp")
    feature_peers = lax.axis_size("mp")
    capacity_old, kinds, columns = master.shape
    width = lane_split(columns, peers)
    features = tokens.shape[1]
    scale_in = features ** (-0.5)
    scale_hidden = (columns * feature_peers) ** (-0.5)

    piece = tokens.shape[0] // feature_peers
    first_row = lax.axis_index("mp") * piece
    mine = jnp.stack(
        [
            lax.dynamic_slice_in_dim(tokens, first_row, piece, 0),
            lax.dynamic_slice_in_dim(upstream, first_row, piece, 0),
        ]
    )
    everyone = lax.all_gather(mine, ("dp", "mp"), axis=1, tiled=True)
    all_tokens, all_upstream = everyone[0], everyone[1]

    weights = master.astype(jnp.bfloat16)
    flat = [grown(weights[:, kind], 1, 0, peers * width - columns) for kind in range(kinds)]
    weights = jnp.stack(
        [
            jnp.concatenate([value[:, peer * width : (peer + 1) * width] for value in flat], 1)
            for peer in range(peers)
        ]
    )
    blocks = lax.all_to_all(weights, "dp", 0, 0)
    blocks = blocks.reshape(peers * capacity_old, kinds * width)
    target, in_range = row_layout(peers * capacity_old, capacity_old, old_offsets)
    target = jnp.where(in_range, target, features)
    wanted = jnp.arange(features, dtype=jnp.int32)[:, None] == target[None, :]
    rows = product(wanted.astype(jnp.bfloat16), blocks, 1, 0).astype(jnp.bfloat16)
    rows = lax.optimization_barrier(rows)
    rows = [rows[:, kind * width : (kind + 1) * width] for kind in range(kinds)]

    gate_act = product(all_tokens, rows[0], 1, 0) * scale_in
    up_act = product(all_tokens, rows[1], 1, 0) * scale_in
    back_grad = product(all_upstream, rows[2], 1, 0) * scale_hidden
    sigmoid_gate = jax.nn.sigmoid(gate_act)
    hidden = (gate_act * sigmoid_gate * up_act).astype(jnp.bfloat16)
    gate_grad = (
        back_grad * up_act * sigmoid_gate * (1.0 + gate_act * (1.0 - sigmoid_gate))
    ).astype(jnp.bfloat16)
    up_grad = (back_grad * gate_act * sigmoid_gate).astype(jnp.bfloat16)

    grads = jnp.concatenate(
        [
            (product(all_tokens, gate_grad, 0, 0) * scale_in).astype(jnp.bfloat16),
            (product(all_tokens, up_grad, 0, 0) * scale_in).astype(jnp.bfloat16),
            (product(all_upstream, hidden, 0, 0) * scale_hidden).astype(jnp.bfloat16),
        ],
        axis=1,
    )
    grads = grown(grads, 0, 0, capacity_new)
    packed = jnp.stack(
        [
            lax.dynamic_slice_in_dim(grads, new_offsets[peer], capacity_new, 0)
            for peer in range(peers)
        ]
    )
    packed = lax.all_to_all(packed, "dp", 0, 0)
    grads = [
        jnp.concatenate(
            [packed[peer, :, kind * width : (kind + 1) * width] for peer in range(peers)], 1
        )[:, :columns]
        for kind in range(kinds)
    ]

    partial_value = (product(hidden, rows[2], 1, 1) * scale_hidden).astype(jnp.bfloat16)
    partial_value = lax.psum_scatter(partial_value, "mp", scatter_dimension=1, tiled=True)
    layer_output = lax.psum_scatter(partial_value, "dp", scatter_dimension=0, tiled=True)
    return jnp.stack(grads).astype(jnp.float32), layer_output


def token_body(*arguments):
    return token_step(*arguments)


def token_step(tokens, out_grad, master, moment_one, moment_two, old_offsets, new_offsets):
    devices = lax.axis_size("dp")
    capacity_old = master.shape[0]
    capacity_new = new_capacity(tokens.shape[1], devices)
    device_index = lax.axis_index("dp")
    new_start = lookup(new_offsets, device_index)
    new_end = lookup(new_offsets, device_index + 1)
    old_start = lookup(old_offsets, device_index)
    left_start = lookup(old_offsets, jnp.maximum(device_index - 1, 0))
    live_flag = new_end != new_start
    upstream = jnp.where(live_flag, out_grad, jnp.zeros_like(out_grad))

    states = [value.transpose(1, 0, 2) for value in (master, moment_one, moment_two)]
    from_left = []
    for value in states:
        from_left.append(passed_along(value.astype(jnp.bfloat16), "dp", 1))
    grads, layer_output = token_pass(
        tokens, upstream, master, old_offsets, new_offsets, capacity_new
    )
    arrived = jnp.clip(old_start - new_start, 0, capacity_new)
    left_skip = jnp.clip(new_start - left_start, 0, capacity_old)
    slot = jnp.arange(capacity_new, dtype=jnp.int32)[None, :, None]

    def placed(own, left):
        left = lax.dynamic_slice_in_dim(grown(left, 1, 0, capacity_new), left_skip, capacity_new, 1)
        own = grown(own, 1, capacity_new, capacity_new - capacity_old)
        own = lax.dynamic_slice_in_dim(own, capacity_new - arrived, capacity_new, 1)
        return jnp.where(slot < arrived, left.astype(jnp.float32), own)

    rows = [placed(own, left) for own, left in zip(states, from_left)]
    updated = adam_step(rows[0], rows[1], rows[2], grads)
    in_range = slot < new_end - new_start
    updated = [jnp.where(in_range, value, 0.0).transpose(1, 0, 2) for value in updated]
    layer_output = jnp.where(live_flag, layer_output, jnp.zeros_like(layer_output))
    return (updated[0], updated[1], updated[2], layer_output)


def new_capacity(features, devices):
    shard_rows = features // devices
    jitter_rows = shard_rows // (2 * (devices - 1)) + 2
    return shard_rows + shard_rows // 4 + 2 * jitter_rows


def any_body(tokens, out_grad, master, *others):
    devices = lax.axis_size("dp")
    columns = master.shape[2]
    moved_tokens = 3 * tokens.shape[0] * devices
    moved_rows = 2 * master.shape[1] * columns
    whole = tokens.shape[0] % lax.axis_size("mp") == 0
    chosen = token_body if whole and moved_tokens <= moved_rows else body
    return chosen(tokens, out_grad, master, *others)


def solution(mesh):
    placed = (
        P("dp", None),
        P("dp", None),
        P("dp", None, "mp"),
        P("dp", None, "mp"),
        P("dp", None, "mp"),
        P(),
        P(),
    )
    return jax.shard_map(
        any_body,
        mesh=mesh,
        in_specs=placed,
        out_specs=(P("dp", None, "mp"), P("dp", None, "mp"), P("dp", None, "mp"), P("dp", "mp")),
        check_vma=False,
    )
```

```python
import jax
import jax.numpy as jnp
from jax import lax
from jax.sharding import PartitionSpec as P


FEATURE_WIDTH = 2048
FF = 7168


beta_one = 0.9
beta_two = 0.95
learn_rate = 0.01
decay_rate = 0.1
adam_eps = 1e-08
bias_one = 1.0 - 0.9**10
bias_two = 1.0 - 0.95**10


def passed_along(value, axis, by):
    peers = lax.axis_size(axis)
    pairs = [(i, i + by) for i in range(peers) if 0 <= i + by < peers]
    return lax.ppermute(value, axis, pairs)


def lookup(small_table, wanted):
    matches = wanted[..., None] == jnp.arange(small_table.shape[0], dtype=jnp.int32)
    return jnp.sum(jnp.where(matches, small_table, 0), axis=-1)


def row_layout(row_count, capacity, offsets):
    row_index = jnp.arange(row_count, dtype=jnp.int32)
    owner_index = row_index // capacity
    local_index = row_index - owner_index * capacity
    row_start = lookup(offsets, owner_index)
    in_range = local_index < lookup(offsets, owner_index + 1) - row_start
    target = jnp.clip(row_start + local_index, 0, FEATURE_WIDTH - 1)
    return (target, in_range)


def adam_step(master_rows, first_rows, second_rows, grads):
    first_new = beta_one * first_rows + (1.0 - beta_one) * grads
    second_new = beta_two * second_rows + (1.0 - beta_two) * grads * grads
    update = first_new / bias_one / (jnp.sqrt(second_new / bias_two) + adam_eps)
    master_new = master_rows - learn_rate * (update + decay_rate * master_rows)
    return (master_new, first_new, second_new)


def reshard(states, old_offsets, new_offsets, capacity_new):
    capacity_old = states.shape[0]
    from_left = passed_along(states.astype(jnp.bfloat16), "dp", 1).astype(states.dtype)
    device_index = lax.axis_index("dp")
    local_index = jnp.arange(capacity_new, dtype=jnp.int32)
    row_start = lookup(new_offsets, device_index)
    row_count = lookup(new_offsets, device_index + 1) - row_start
    in_range = local_index < row_count
    row_index = jnp.clip(row_start + local_index, 0, FEATURE_WIDTH - 1)
    owner_index = jnp.sum(
        (old_offsets[1:-1][None, :] <= row_index[:, None]).astype(jnp.int32), axis=1
    )
    slot_index = (
        (owner_index - device_index + 1) * capacity_old
        + row_index
        - lookup(old_offsets, owner_index)
    )
    neighbours = jnp.concatenate([from_left, states], axis=0)
    picked = jnp.take(neighbours, slot_index, axis=0, mode="clip")
    return jnp.where(in_range[:, None, None, None], picked, 0.0)


def train_pass(tokens, upstream, weights, layout, capacity, live_flag):
    columns = weights.shape[2]
    scale_in = FEATURE_WIDTH ** (-0.5)
    scale_hidden = FF ** (-0.5)
    contract_rows = (((0,), (0,)), ((), ()))
    shard_piece = lax.all_gather(weights, "dp", axis=0, tiled=True)
    down_rows = jnp.zeros((FEATURE_WIDTH, columns), jnp.bfloat16)
    target, in_range = row_layout(shard_piece.shape[0], capacity, layout)
    shard_piece = jnp.where(in_range[:, None, None], shard_piece, jnp.zeros_like(shard_piece))
    token_columns = jnp.take(tokens, target, axis=1, mode="clip")
    upstream_columns = jnp.take(upstream, target, axis=1, mode="clip")
    gate_sum = jnp.dot(token_columns, shard_piece[:, 0], preferred_element_type=jnp.float32)
    up_sum = jnp.dot(token_columns, shard_piece[:, 1], preferred_element_type=jnp.float32)
    back_sum = jnp.dot(upstream_columns, shard_piece[:, 2], preferred_element_type=jnp.float32)
    placed = jnp.where(in_range, target, FEATURE_WIDTH)
    down_rows = down_rows.at[placed].set(shard_piece[:, 2], mode="drop")
    gate_sum, up_sum, back_sum, down_rows = (gate_sum, up_sum, back_sum, down_rows)
    gate_act = gate_sum * scale_in
    up_act = up_sum * scale_in
    back_grad = back_sum * scale_hidden
    sigmoid_gate = jax.nn.sigmoid(gate_act)
    hidden = (gate_act * sigmoid_gate * up_act).astype(jnp.bfloat16)
    partial_value = (
        lax.dot_general(
            hidden, down_rows, (((1,), (1,)), ((), ())), preferred_element_type=jnp.float32
        )
        * scale_hidden
    )
    partial_value = jnp.where(live_flag, partial_value, 0.0)
    layer_output = lax.psum_scatter(
        partial_value.astype(jnp.bfloat16), "mp", scatter_dimension=1, tiled=True
    )
    gate_grad = (
        back_grad * up_act * sigmoid_gate * (1.0 + gate_act * (1.0 - sigmoid_gate))
    ).astype(jnp.bfloat16)
    up_grad = (back_grad * gate_act * sigmoid_gate).astype(jnp.bfloat16)
    target, in_range = row_layout(lax.axis_size("dp") * capacity, capacity, layout)
    token_columns = jnp.take(tokens, target, axis=1, mode="clip")
    upstream_columns = jnp.take(upstream, target, axis=1, mode="clip")
    gate_part = (
        lax.dot_general(token_columns, gate_grad, contract_rows, preferred_element_type=jnp.float32)
        * scale_in
    )
    up_part = (
        lax.dot_general(token_columns, up_grad, contract_rows, preferred_element_type=jnp.float32)
        * scale_in
    )
    down_part = (
        lax.dot_general(upstream_columns, hidden, contract_rows, preferred_element_type=jnp.float32)
        * scale_hidden
    )
    stacked = jnp.stack([gate_part, up_part, down_part], axis=1)
    grads = lax.psum_scatter(
        jnp.where(in_range[:, None, None], stacked, 0.0).astype(jnp.bfloat16),
        "dp",
        scatter_dimension=0,
        tiled=True,
    ).astype(jnp.float32)
    return (grads, layer_output)


def body(tokens, out_grad, master, moment_one, moment_two, old_offsets, new_offsets):
    devices = lax.axis_size("dp")
    shard_rows = FEATURE_WIDTH // devices
    jitter_rows = shard_rows // (2 * (devices - 1)) + 2
    capacity_new = shard_rows + shard_rows // 4 + 2 * jitter_rows
    device_index = lax.axis_index("dp")
    live_flag = lookup(new_offsets, device_index + 1) != lookup(new_offsets, device_index)
    upstream = jnp.where(live_flag, out_grad, jnp.zeros_like(out_grad))
    states = jnp.stack([master, moment_one, moment_two], axis=1)
    weights = states[:, 0].astype(jnp.bfloat16)
    grads, layer_output = train_pass(
        tokens, upstream, weights, old_offsets, states.shape[0], live_flag
    )
    updated = jnp.stack(adam_step(states[:, 0], states[:, 1], states[:, 2], grads), axis=1)
    updated = reshard(updated, old_offsets, new_offsets, capacity_new)
    return (updated[:, 0], updated[:, 1], updated[:, 2], layer_output)


def grown(value, axis, before, after):
    widths = [(0, 0)] * value.ndim
    widths[axis] = (before, after)
    return jnp.pad(value, widths)


def lane_split(columns, peers):
    return -(-columns // (peers * 128)) * 128


def product(left, right, left_dim, right_dim):
    return lax.dot_general(
        left,
        right,
        (((left_dim,), (right_dim,)), ((), ())),
        preferred_element_type=jnp.float32,
    )


def token_pass(tokens, upstream, master, old_offsets, new_offsets, capacity_new):
    peers = lax.axis_size("dp")
    feature_peers = lax.axis_size("mp")
    capacity_old, kinds, columns = master.shape
    width = lane_split(columns, peers)
    features = tokens.shape[1]
    scale_in = features ** (-0.5)
    scale_hidden = (columns * feature_peers) ** (-0.5)

    piece = tokens.shape[0] // feature_peers
    first_row = lax.axis_index("mp") * piece

    def everyone(value):
        mine = lax.dynamic_slice_in_dim(value, first_row, piece, 0)
        return lax.all_gather(mine, ("dp", "mp"), axis=0, tiled=True)

    all_tokens = everyone(tokens)
    all_upstream = everyone(upstream)

    weights = master.astype(jnp.bfloat16)
    flat = [grown(weights[:, kind], 1, 0, peers * width - columns) for kind in range(kinds)]
    weights = jnp.stack(
        [
            jnp.concatenate([value[:, peer * width : (peer + 1) * width] for value in flat], 1)
            for peer in range(peers)
        ]
    )
    blocks = lax.all_to_all(weights, "dp", 0, 0)
    blocks = blocks.reshape(peers * capacity_old, kinds * width)
    target, in_range = row_layout(peers * capacity_old, capacity_old, old_offsets)
    target = jnp.where(in_range, target, features)
    wanted = jnp.arange(features, dtype=jnp.int32)[:, None] == target[None, :]
    rows = product(wanted.astype(jnp.bfloat16), blocks, 1, 0).astype(jnp.bfloat16)
    rows = lax.optimization_barrier(rows)
    rows = [rows[:, kind * width : (kind + 1) * width] for kind in range(kinds)]

    gate_act = product(all_tokens, rows[0], 1, 0) * scale_in
    up_act = product(all_tokens, rows[1], 1, 0) * scale_in
    back_grad = product(all_upstream, rows[2], 1, 0) * scale_hidden
    sigmoid_gate = jax.nn.sigmoid(gate_act)
    hidden = (gate_act * sigmoid_gate * up_act).astype(jnp.bfloat16)
    gate_grad = (
        back_grad * up_act * sigmoid_gate * (1.0 + gate_act * (1.0 - sigmoid_gate))
    ).astype(jnp.bfloat16)
    up_grad = (back_grad * gate_act * sigmoid_gate).astype(jnp.bfloat16)

    grads = jnp.concatenate(
        [
            (product(all_tokens, gate_grad, 0, 0) * scale_in).astype(jnp.bfloat16),
            (product(all_tokens, up_grad, 0, 0) * scale_in).astype(jnp.bfloat16),
            (product(all_upstream, hidden, 0, 0) * scale_hidden).astype(jnp.bfloat16),
        ],
        axis=1,
    )
    target, in_range = row_layout(peers * capacity_new, capacity_new, new_offsets)
    target = jnp.where(in_range, target, features)
    wanted = target[:, None] == jnp.arange(features, dtype=jnp.int32)[None, :]
    grads = lax.optimization_barrier(grads)
    packed = product(wanted.astype(jnp.bfloat16), grads, 1, 0).astype(jnp.bfloat16)
    packed = packed.reshape(peers, capacity_new, kinds * width)
    packed = lax.all_to_all(packed, "dp", 0, 0)
    grads = [
        jnp.concatenate(
            [packed[peer, :, kind * width : (kind + 1) * width] for peer in range(peers)], 1
        )[:, :columns]
        for kind in range(kinds)
    ]

    partial_value = (product(hidden, rows[2], 1, 1) * scale_hidden).astype(jnp.bfloat16)
    partial_value = lax.psum_scatter(partial_value, "mp", scatter_dimension=1, tiled=True)
    shares = partial_value.reshape(peers, -1, partial_value.shape[1])
    shares = lax.all_to_all(shares, "dp", 0, 0)
    layer_output = jnp.sum(shares.astype(jnp.float32), axis=0).astype(jnp.bfloat16)
    return jnp.stack(grads).astype(jnp.float32), layer_output


def token_body(*arguments):
    return token_step(*arguments)


def token_step(tokens, out_grad, master, moment_one, moment_two, old_offsets, new_offsets):
    devices = lax.axis_size("dp")
    capacity_old = master.shape[0]
    capacity_new = new_capacity(tokens.shape[1], devices)
    device_index = lax.axis_index("dp")
    new_start = lookup(new_offsets, device_index)
    new_end = lookup(new_offsets, device_index + 1)
    old_start = lookup(old_offsets, device_index)
    left_start = lookup(old_offsets, jnp.maximum(device_index - 1, 0))
    live_flag = new_end != new_start
    upstream = jnp.where(live_flag, out_grad, jnp.zeros_like(out_grad))

    states = [value.transpose(1, 0, 2) for value in (master, moment_one, moment_two)]
    from_left = []
    for value in states:
        from_left.append(passed_along(value.astype(jnp.bfloat16), "dp", 1))
    grads, layer_output = token_pass(
        tokens, upstream, master, old_offsets, new_offsets, capacity_new
    )
    arrived = jnp.clip(old_start - new_start, 0, capacity_new)
    left_skip = jnp.clip(new_start - left_start, 0, capacity_old)
    slot = jnp.arange(capacity_new, dtype=jnp.int32)[None, :, None]

    def placed(own, left):
        left = lax.dynamic_slice_in_dim(grown(left, 1, 0, capacity_new), left_skip, capacity_new, 1)
        own = grown(own, 1, capacity_new, capacity_new - capacity_old)
        own = lax.dynamic_slice_in_dim(own, capacity_new - arrived, capacity_new, 1)
        return jnp.where(slot < arrived, left.astype(jnp.float32), own)

    rows = [placed(own, left) for own, left in zip(states, from_left)]
    updated = adam_step(rows[0], rows[1], rows[2], grads)
    in_range = slot < new_end - new_start
    updated = [jnp.where(in_range, value, 0.0).transpose(1, 0, 2) for value in updated]
    layer_output = jnp.where(live_flag, layer_output, jnp.zeros_like(layer_output))
    return (updated[0], updated[1], updated[2], layer_output)


def new_capacity(features, devices):
    shard_rows = features // devices
    jitter_rows = shard_rows // (2 * (devices - 1)) + 2
    return shard_rows + shard_rows // 4 + 2 * jitter_rows


def any_body(tokens, out_grad, master, *others):
    devices = lax.axis_size("dp")
    columns = master.shape[2]
    moved_tokens = 3 * tokens.shape[0] * devices
    moved_rows = 2 * master.shape[1] * columns
    whole = tokens.shape[0] % lax.axis_size("mp") == 0
    chosen = token_body if whole and moved_tokens <= moved_rows else body
    return chosen(tokens, out_grad, master, *others)


def solution(mesh):
    placed = (
        P("dp", None),
        P("dp", None),
        P("dp", None, "mp"),
        P("dp", None, "mp"),
        P("dp", None, "mp"),
        P(),
        P(),
    )
    return jax.shard_map(
        any_body,
        mesh=mesh,
        in_specs=placed,
        out_specs=(P("dp", None, "mp"), P("dp", None, "mp"), P("dp", None, "mp"), P("dp", "mp")),
        check_vma=False,
    )
```
